128 devices in a mesh: gx: 8 (over z, core), gy: 16 (over x, y).
Axes of the slice: x: 4, y: 4, z: 4, core: 2. Of those that a mesh axis runs over, the one named last changes fastest.
Arguments:
- conductivity: float32 [16, 512, 2048], P(None, 'gx', 'gy'), may hold values from 0.1 to 10
- well_rates: float32 [16, 512, 2048], P(None, 'gx', 'gy'), may hold values from -384 to 384
- block_label: int32 [512, 2048], P('gx', 'gy'), may hold values from 0 to 1023, as said below
- owned_pairs: int32 [1024], P(('gx', 'gy')), may hold values from 0 to 1023, each once
Outputs:
- fine_flux: float32 [3, 16, 512, 2048], P(None, None, 'gx', 'gy')
- coarse_flux: float32 [1024], P(('gx', 'gy'))
The draws below stay inside these ranges and needn't reach their ends.
Inputs may be any that keep to these rules, and one draw needn't show every extreme that they name: `block_label`: label = column * 64 + row, with column = ((x + o) // 32) % 16 for an offset o of 0 to 31 that is fixed for each fine row y, and row = ((y + q) // 32) % 64 for an offset q of 0 to 31 that is fixed for each fine column x. `owned_pairs`: each pair number once; the pairs in one device's shard are owned by that device.
All inputs are finite; a program needn't handle non-finite values.
Results may differ from the reference program's by a relative error of at most 0.0003.
Values sent between devices are 32-bit elements; how exact they have to be, the bound alone decides.
A program may use at most 128 MiB of HBM per device.

```python
import math
import jax
import jax.numpy as jnp
from jax import lax

NZ = 16
BX = 32
BY = 32
ITERS = 13
NX = 512
NY = 2048
NBX = 16
NBY = 64
PAIRS = 1024


def draw_block_label(key, part):
    row_key = jax.random.fold_in(key, 11)
    column_key = jax.random.fold_in(key, 23)
    offsets = jax.random.randint(row_key, (NY,), 0, BX)
    shifts = jax.random.randint(column_key, (NX,), 0, BY)
    column = (jnp.arange(NX)[:, None] + offsets[None, :]) // BX % NBX
    row_index = (jnp.arange(NY)[None, :] + shifts[:, None]) // BY % NBY
    return (column * NBY + row_index).astype(jnp.int32)


def level_of(key, shape, shards, least, high):
    loudness = 1.0
    for axis_at, parts in shards:
        heights = jax.random.uniform(jax.random.fold_in(jax.random.fold_in(key, 6), axis_at), (parts,), jnp.float32, least / len(shards), high / len(shards))
        loudness = loudness * jnp.repeat(jnp.exp(heights), shape[axis_at] // parts).reshape((-1,) + (1,) * (len(shape) - 1 - axis_at))
    return loudness


def noise(own_key, dims, scale, bound, split=(), held_as=jnp.bfloat16):
    entries = scale * jax.random.normal(own_key, dims, jnp.float32)
    if split:
        entries = entries * level_of(own_key, dims, split, -0.22, 0.18)
    return jnp.clip(entries, -bound, bound).astype(held_as)


def setup_inputs(seed: int = 0) -> dict:
    streams_of = jax.random.split(jax.random.key(seed), 5)
    conductivity = jnp.clip(jnp.exp(math.log(10.0) - 4.6051702 * jax.random.uniform(streams_of[0], (NZ, NX, NY), jnp.float32) ** level_of(streams_of[0], (NZ, NX, NY), ((1, 8), (2, 16)), -0.2, 0.2)), 0.1, 10.0)
    well_rates = noise(streams_of[1], (NZ, NX, NY), (2 * BX), 384.0, ((1, 8), (2, 16)), jnp.float32)
    block_label = draw_block_label(jax.random.fold_in(streams_of[4], 71), 0)
    owned_pairs = jax.random.permutation(streams_of[3], PAIRS).astype(jnp.int32)
    return dict(conductivity=conductivity, well_rates=well_rates, block_label=block_label, owned_pairs=owned_pairs)


REACTION = 0.05
RELAXATION = 0.8


def harmonic(one_side, other_side):
    total = one_side + other_side
    return 2.0 * one_side * other_side / jnp.where(total > 0, total, 1.0)


def pair_fields(labels_grid, blocks_x, blocks_y):
    column = labels_grid // blocks_y
    row_index = labels_grid % blocks_y
    first_ids = (column // 2) * blocks_y + row_index
    second_ids = (((column + blocks_x - 1) % blocks_x) // 2) * blocks_y + row_index + (blocks_x // 2) * blocks_y
    parity_sign = jnp.where(column % 2 == 0, 1.0, -1.0).astype(jnp.float32)
    return jnp.stack([first_ids, second_ids]).astype(jnp.int32), jnp.stack([parity_sign, -parity_sign])


def shift_up(field):
    return jnp.concatenate([field[:, 1:], jnp.zeros_like(field[:, :1])], axis=1)


def shift_down(field):
    return jnp.concatenate([jnp.zeros_like(field[:, :1]), field[:, :-1]], axis=1)


def reference(conductivity, well_rates, block_label, owned_pairs):
    pair_ids, signs = pair_fields(block_label, NBX, NBY)
    same_x = pair_ids == jnp.roll(pair_ids, -1, axis=1)
    same_y = pair_ids == jnp.roll(pair_ids, -1, axis=2)
    trans_x = jnp.where(same_x[:, None], harmonic(conductivity, jnp.roll(conductivity, -1, axis=1))[None], 0.0)
    trans_y = jnp.where(same_y[:, None], harmonic(conductivity, jnp.roll(conductivity, -1, axis=2))[None], 0.0)
    vertical = harmonic(conductivity[:-1], conductivity[1:])
    flat_layer = jnp.zeros((1, NX, NY), jnp.float32)
    trans_up = jnp.concatenate([vertical, flat_layer], axis=0)
    trans_down = jnp.concatenate([flat_layer, vertical], axis=0)
    back_x = jnp.roll(trans_x, 1, axis=2)
    back_y = jnp.roll(trans_y, 1, axis=3)
    diagonal = REACTION + trans_x + back_x + trans_y + back_y + trans_up + trans_down
    source = jnp.broadcast_to(signs[:, None], diagonal.shape)

    def sweep(sweep_index, pressure):
        applied = (REACTION * pressure
                   + trans_x * (pressure - jnp.roll(pressure, -1, axis=2))
                   + back_x * (pressure - jnp.roll(pressure, 1, axis=2))
                   + trans_y * (pressure - jnp.roll(pressure, -1, axis=3))
                   + back_y * (pressure - jnp.roll(pressure, 1, axis=3))
                   + trans_up * (pressure - shift_up(pressure))
                   + trans_down * (pressure - shift_down(pressure)))
        return pressure + RELAXATION * (source - applied) / diagonal

    pressure = lax.fori_loop(0, ITERS, sweep, jnp.zeros(diagonal.shape, jnp.float32))
    diff_x = pressure - jnp.roll(pressure, -1, axis=2)
    diff_y = pressure - jnp.roll(pressure, -1, axis=3)
    diff_z = pressure - shift_up(pressure)
    flux_x = trans_x * diff_x
    flux_y = trans_y * diff_y
    flux_z = trans_up * diff_z
    energy = jnp.sum(flux_x * diff_x + flux_y * diff_y + flux_z * diff_z + REACTION * pressure * pressure, axis=1)
    load_cell = jnp.sum(well_rates[None] * pressure, axis=1)
    flat_ids = pair_ids.reshape(-1)
    energy_sum = jax.ops.segment_sum(energy.reshape(-1), flat_ids, num_segments=PAIRS)
    load_sum = jax.ops.segment_sum(load_cell.reshape(-1), flat_ids, num_segments=PAIRS)
    all_rates = load_sum / energy_sum
    coarse_flux = jnp.take(all_rates, owned_pairs)
    weight = jnp.take(all_rates, pair_ids)[:, None]
    fine_flux = jnp.stack([jnp.sum(weight * flux_x, axis=0), jnp.sum(weight * flux_y, axis=0), jnp.sum(weight * flux_z, axis=0)])
    return fine_flux, coarse_flux
```

```python
import functools

import jax
import jax.numpy as jnp
from jax import lax
from jax.experimental import pallas as pl
from jax.experimental.pallas import tpu as pltpu
from jax.sharding import PartitionSpec as P

ITERS = 13
REACTION = 0.05
RELAXATION = 0.8
NZ = 16
CX = 64
CY = 128
HALO = 16
EXT = CX + 2 * HALO
PAD = 8
ROWS = EXT + 2 * PAD
NBINS = 10
MESH = pl.DeviceIdType.MESH
f32 = jnp.float32


def lane_iota():
    return lax.broadcasted_iota(jnp.int32, (8, 128), 1)


def roll(value, shift):
    return pltpu.roll(value, shift % 128, 1)


class Seams:
    def __init__(self):
        lane = lane_iota()
        self.group = ((lane + 16) & 127) >> 5
        inner = lane & 31
        self.first = [lane == 32 * g for g in range(4)]
        self.last = [lane == (32 * g - 1) % 128 for g in range(4)]
        self.any_first = inner == 0
        self.any_last = inner == 31
        self.right_half = inner < 16

    def compose(self, own):
        return jnp.where(
            self.group < 2,
            jnp.where(self.group < 1, own[0], own[1]),
            jnp.where(self.group < 3, own[2], own[3]),
        )

    def right(self, own, strip, mixed):
        out = [roll(jnp.where(self.first[g], strip, own[g]), -1) for g in range(4)]
        return out, roll(jnp.where(self.any_first, mixed, strip), -1)

    def left(self, own, strip, mixed):
        out = [roll(jnp.where(self.last[g], strip, own[g]), 1) for g in range(4)]
        return out, roll(jnp.where(self.any_last, mixed, strip), 1)


def both_sides(seams, own20, left=True):
    right, lefts = [None] * 20, [None] * 20
    for k in range(4):
        own = [own20[4 * g + k] for g in range(4)]
        strip = own20[16 + k]
        mixed = seams.compose(own)
        out, edge = seams.right(own, strip, mixed)
        for g in range(4):
            right[4 * g + k] = out[g]
        right[16 + k] = edge
        if left:
            out, edge = seams.left(own, strip, mixed)
            for g in range(4):
                lefts[4 * g + k] = out[g]
            lefts[16 + k] = edge
    return right, lefts


def plane_of(i):
    return i // 4 if i < 16 else 4


def layer_above(values, i):
    if i % 4 != 3:
        return values[i + 1]
    return roll(values[i + 1 if i < NZ - 1 else 16 if i == 19 else 0], -32)


def layer_below(values, i):
    if i % 4 != 0:
        return values[i - 1]
    return roll(values[19 if i == 16 else i - 1], 32)


def harmonic(one, other):
    return 2.0 * one * other / (one + other)


def pair_ids(label, row_bits, columns):
    column = label >> row_bits
    row = label & ((1 << row_bits) - 1)
    first = ((column >> 1) << row_bits) + row
    second = ((((column + columns - 1) & (columns - 1)) >> 1) << row_bits) + row + ((columns // 2) << row_bits)
    sign = jnp.where((column & 1) == 0, 1.0, -1.0).astype(f32)
    return first, second, sign


def kernel(gx, gy, cond, well, label, owned, fine, coarse, ce, le, wl, send_l, send_r, from_l, from_r,
           c, ids, tx, ty, tyb, hz, hzb, w, s, p, flux, sums, part, gathered, staged,
           local_sem, out_sem, halo_send, halo_recv, row_send, row_recv, col_send, col_recv):
    m, n = lax.axis_index("gx"), lax.axis_index("gy")
    row_bits = (4 * gy).bit_length() - 1
    columns = 2 * gx

    def at(dm, dn):
        return (lax.rem(m + dm + gx, gx), lax.rem(n + dn + gy, gy))

    partners = [at(d, 0) for d in range(1, gx)] + [at(0, d) for d in range(1, gy)]
    partners += [at(a, b) for a in (-1, 1) for b in (-1, 1)]
    barrier = pltpu.get_barrier_semaphore()
    for partner in partners:
        pl.semaphore_signal(barrier, inc=1, device_id=partner, device_id_type=MESH)

    own_rows = pl.ds(HALO, CX)
    loads = [
        pltpu.make_async_copy(cond, ce.at[:, own_rows], local_sem.at[0]),
        pltpu.make_async_copy(label, le.at[own_rows], local_sem.at[1]),
        pltpu.make_async_copy(well, wl, local_sem.at[2]),
    ]
    for load in loads:
        load.start()

    for f in range(2):
        tx[f, :, :PAD, :] = jnp.zeros((20, PAD, 128), f32)
        for slot in range(2):
            p[slot, f, :, :PAD, :] = jnp.zeros((20, PAD, 128), f32)
            p[slot, f, :, ROWS - PAD :, :] = jnp.zeros((20, PAD, 128), f32)
        for plane in range(5):
            ids[f, plane, ROWS - PAD :, :] = jnp.zeros((PAD, 128), jnp.int32)
    c[:, ROWS - PAD :, :] = jnp.ones((20, PAD, 128), f32)

    loads[0].wait()
    loads[1].wait()

    def pack(xb, carry):
        seams = Seams()
        rows = pl.ds(pl.multiple_of(HALO + 8 * xb, 8), 8)
        out = pl.ds(pl.multiple_of(8 * xb, 8), 8)
        mixed = [
            seams.compose([roll(ce[4 * g + k, rows, :], 32 * g) for g in range(4)]) for k in range(4)
        ]
        for h in range(2):
            even, odd = mixed[2 * h], roll(mixed[2 * h + 1], 16)
            send_l[h, out, :] = jnp.where(seams.right_half, even, odd)
            send_r[h, out, :] = jnp.where(seams.right_half, odd, even)
        tags = seams.compose([roll(le[rows, :], 32 * g) for g in range(4)]).astype(f32)
        send_l[2, out, :] = tags
        send_r[2, out, :] = tags
        return carry

    lax.fori_loop(0, CX // 8, pack, 0)
    pl.semaphore_wait(barrier, len(partners))

    low, high = pl.ds(0, HALO), pl.ds(CX - HALO, HALO)
    below, above = pl.ds(0, HALO), pl.ds(HALO + CX, HALO)
    moves = [
        (cond.at[:, low], ce.at[:, above], at(-1, 0)),
        (cond.at[:, high], ce.at[:, below], at(1, 0)),
        (label.at[low], le.at[above], at(-1, 0)),
        (label.at[high], le.at[below], at(1, 0)),
        (send_l, from_r.at[:, own_rows], at(0, -1)),
        (send_r, from_l.at[:, own_rows], at(0, 1)),
        (send_l.at[:, low], from_r.at[:, above], at(-1, -1)),
        (send_l.at[:, high], from_r.at[:, below], at(1, -1)),
        (send_r.at[:, low], from_l.at[:, above], at(-1, 1)),
        (send_r.at[:, high], from_l.at[:, below], at(1, 1)),
    ]
    halos = [
        pltpu.make_async_remote_copy(src, dst, halo_send.at[i], halo_recv.at[i], device_id=to, device_id_type=MESH)
        for i, (src, dst, to) in enumerate(moves)
    ]
    for halo in halos:
        halo.start()
    for halo in halos:
        halo.wait()

    def assemble(xb, carry):
        seams = Seams()
        rows = pl.ds(pl.multiple_of(8 * xb, 8), 8)
        out = pl.ds(pl.multiple_of(PAD + 8 * xb, 8), 8)
        for z in range(NZ):
            c[z, out, :] = roll(ce[z, rows, :], 32 * (z // 4))
        for h in range(2):
            right, left = from_r[h, rows, :], from_l[h, rows, :]
            c[16 + 2 * h, out, :] = jnp.where(seams.right_half, right, left)
            c[17 + 2 * h, out, :] = jnp.where(seams.right_half, roll(right, -16), roll(left, -16))
        tags = jnp.where(seams.right_half, from_r[2, rows, :], from_l[2, rows, :]).astype(jnp.int32)
        labels = [roll(le[rows, :], 32 * g) for g in range(4)] + [tags]
        for plane in range(5):
            first, second, sign = pair_ids(labels[plane], row_bits, columns)
            ids[0, plane, out, :] = first
            ids[1, plane, out, :] = second
            s[0, plane, out, :] = sign
            s[1, plane, out, :] = -sign
        return carry

    lax.fori_loop(0, EXT // 8, assemble, 0)

    def faces(xb, carry):
        seams = Seams()
        a = PAD + 8 * xb
        here, ahead = pl.ds(pl.multiple_of(a, 8), 8), pl.ds(a + 1, 8)
        cs = [c[i, here, :] for i in range(20)]
        right, _ = both_sides(seams, cs, left=False)
        hx = [harmonic(cs[i], c[i, ahead, :]) for i in range(20)]
        hy = [harmonic(cs[i], right[i]) for i in range(20)]
        for i in range(20):
            face = jnp.zeros((8, 128), f32)
            if i != NZ - 1:
                face = harmonic(cs[i], layer_above(cs, i))
            if i == 19:
                face = jnp.where(seams.group == 3, 0.0, face)
            hz[i, here, :] = face
            if i % 4 == 3 and i != NZ - 1:
                hzb[i // 4, here, :] = roll(face, 32)
        for f in range(2):
            pid = [ids[f, plane, here, :] for plane in range(5)]
            same_x = [pid[plane] == ids[f, plane, ahead, :] for plane in range(5)]
            out, edge = seams.right(pid[:4], pid[4], seams.compose(pid[:4]))
            same_y = [one == other for one, other in zip(pid, out + [edge])]
            tys = [jnp.where(same_y[plane_of(i)], hy[i], 0.0) for i in range(20)]
            _, back = both_sides(seams, tys)
            for i in range(20):
                tx[f, i, here, :] = jnp.where(same_x[plane_of(i)], hx[i], 0.0)
                ty[f, i, here, :] = tys[i]
                tyb[f, i, here, :] = back[i]
        return carry

    lax.fori_loop(0, EXT // 8, faces, 0)

    def face_below(i, here):
        if i % 4 != 0:
            return hz[i - 1, here, :]
        return hzb[4 if i == 16 else i // 4 - 1, here, :]

    def weights(xb, carry):
        a = PAD + 8 * xb
        here, behind = pl.ds(pl.multiple_of(a, 8), 8), pl.ds(a - 1, 8)
        for f in range(2):
            for i in range(20):
                total = tx[f, i, here, :] + tx[f, i, behind, :] + ty[f, i, here, :] + tyb[f, i, here, :]
                total += hz[i, here, :] + REACTION
                if i != 0:
                    total += face_below(i, here)
                scale = RELAXATION / total
                w[f, i, here, :] = scale
                p[0, f, i, here, :] = s[f, plane_of(i), here, :] * scale
        return carry

    lax.fori_loop(0, EXT // 8, weights, 0)

    def sweep(src, first, last):
        def step(it, carry):
            f, xb = it & 1, first + (it >> 1)
            seams = Seams()
            a = PAD + 8 * xb
            here, ahead, behind = pl.ds(pl.multiple_of(a, 8), 8), pl.ds(a + 1, 8), pl.ds(a - 1, 8)
            ps = [p[src, f, i, here, :] for i in range(20)]
            right, left = both_sides(seams, ps)
            for i in range(20):
                total = s[f, plane_of(i), here, :]
                total += tx[f, i, here, :] * p[src, f, i, ahead, :]
                total += tx[f, i, behind, :] * p[src, f, i, behind, :]
                total += ty[f, i, here, :] * right[i]
                total += tyb[f, i, here, :] * left[i]
                if i != NZ - 1:
                    total += hz[i, here, :] * layer_above(ps, i)
                if i != 0:
                    total += face_below(i, here) * layer_below(ps, i)
                p[1 - src, f, i, here, :] = (1.0 - RELAXATION) * ps[i] + w[f, i, here, :] * total
            return carry

        lax.fori_loop(0, 2 * (last - first), step, 0)

    for k in range(2, ITERS + 1):
        first = (HALO - (ITERS - k)) // 8
        last = (HALO + CX + (ITERS - k)) // 8 + 1
        sweep(k % 2, first, last)
    done = (ITERS + 1) % 2

    loads[2].wait()

    def fluxes(xb, carry):
        seams = Seams()
        a = PAD + HALO + 8 * xb
        here, ahead = pl.ds(pl.multiple_of(a, 8), 8), pl.ds(a + 1, 8)
        own = pl.ds(pl.multiple_of(8 * xb, 8), 8)
        wells = [roll(wl[z, own, :], 32 * (z // 4)) for z in range(NZ)]
        for f in range(2):
            ps = [p[done, f, i, here, :] for i in range(20)]
            right, _ = both_sides(seams, ps, left=False)
            energy, load = jnp.zeros((8, 128), f32), jnp.zeros((8, 128), f32)
            for g in range(4):
                quarter_energy, quarter_load = None, None
                for z in range(4 * g, 4 * g + 4):
                    dx = ps[z] - p[done, f, z, ahead, :]
                    dy = ps[z] - right[z]
                    vx = tx[f, z, here, :] * dx
                    vy = ty[f, z, here, :] * dy
                    cell = vx * dx + vy * dy + REACTION * ps[z] * ps[z]
                    flux[f, 0, z, own, :] = vx
                    flux[f, 1, z, own, :] = vy
                    if z != NZ - 1:
                        dz = ps[z] - layer_above(ps, z)
                        vz = hz[z, here, :] * dz
                        cell += vz * dz
                    else:
                        vz = jnp.zeros((8, 128), f32)
                    flux[f, 2, z, own, :] = vz
                    rated = wells[z] * ps[z]
                    quarter_energy = cell if quarter_energy is None else quarter_energy + cell
                    quarter_load = rated if quarter_load is None else quarter_load + rated
                energy += roll(quarter_energy, -32 * g)
                load += roll(quarter_load, -32 * g)
            sums[f, 0, own, :] = energy
            sums[f, 1, own, :] = load
        return carry

    lax.fori_loop(0, CX // 8, fluxes, 0)

    def bins_of(xb):
        tags = le[HALO + 8 * xb : HALO + 8 * xb + 8, :]
        column = ((tags >> row_bits) - 2 * m) & (columns - 1)
        row = ((tags & ((1 << row_bits) - 1)) - 4 * n) & ((1 << row_bits) - 1)
        return [jnp.where(column >= edge, 5, 0) + row for edge in (2, 1)]

    totals = [[[jnp.zeros((8, 128), f32) for _ in range(NBINS)] for _ in range(2)] for _ in range(2)]
    for xb in range(CX // 8):
        bins = bins_of(xb)
        for f in range(2):
            cells = [sums[f, q, 8 * xb : 8 * xb + 8, :] for q in range(2)]
            for b in range(NBINS):
                hit = bins[f] == b
                for q in range(2):
                    totals[q][f][b] += jnp.where(hit, cells[q], 0.0)
    line = jnp.zeros((1, 128), f32)
    lane_row = lax.broadcasted_iota(jnp.int32, (1, 128), 1)
    for q in range(2):
        for f in range(2):
            for b in range(NBINS):
                value = jnp.sum(totals[q][f][b], axis=0, keepdims=True)
                value = jnp.sum(value, axis=1, keepdims=True)
                line += jnp.where(lane_row == 20 * q + 10 * f + b, value, 0.0)
    part[0] = line
    mine = n * gx + m
    gathered[pl.ds(mine, 1)] = line[None]

    to_row = [
        pltpu.make_async_remote_copy(
            part, gathered.at[pl.ds(mine, 1)], row_send.at[d], row_recv.at[d], device_id=at(d, 0), device_id_type=MESH
        )
        for d in range(1, gx)
    ]
    for copy in to_row:
        copy.start()
    for copy in to_row:
        copy.wait()
    block = pl.ds(n * gx, gx)
    order = sorted(range(1, gy), key=lambda d: min(d, gy - d))
    to_column = {
        d: pltpu.make_async_remote_copy(
            gathered.at[block], gathered.at[block], col_send.at[d], col_recv.at[d], device_id=at(0, d), device_id_type=MESH
        )
        for d in order
    }
    for d in order:
        to_column[d].start()

    lane_full = lax.broadcasted_iota(jnp.int32, (gx, 128), 1)
    row_full = lax.broadcasted_iota(jnp.int32, (gx, 128), 0)
    entry = lane_full % 20
    family = entry // 10
    column_bin = (entry // 5) & 1
    row_bin = entry % 5

    def rows_of(at_n):
        return jnp.concatenate([gathered[at_n * gx + i] for i in range(gx)], axis=0)

    def across_gx(value):
        before = pltpu.roll(pltpu.roll(value, 1, 0), 128 - 5, 1)
        after = pltpu.roll(pltpu.roll(value, gx - 1, 0), 5, 1)
        return value + jnp.where(family == 0, before, after)

    def rates_of(value, previous):
        whole = value + jnp.where(row_bin == 0, pltpu.roll(previous, 128 - 4, 1), 0.0)
        load = pltpu.roll(whole, 128 - 20, 1)
        valid = (lane_full < 20) & (column_bin == family) & (row_bin < 4)
        return jnp.where(valid, load / jnp.where(valid, whole, 1.0), 0.0), valid

    to_column[1].wait_recv()
    to_column[gy - 1].wait_recv()
    wrap = lambda i: lax.rem(i + gy, gy)
    around = [across_gx(rows_of(wrap(n + d))) for d in (-1, 0, 1)]
    rate_here, _ = rates_of(around[1], around[0])
    rate_next, _ = rates_of(around[2], around[1])

    def pick(table, dm, lane):
        hit = (row_full == lax.rem(m + dm + gx, gx)) & (lane_full == lane)
        value = jnp.sum(jnp.where(hit, table, 0.0), axis=0, keepdims=True)
        return jnp.sum(value, axis=1, keepdims=True)

    local = []
    for f in range(2):
        for b in range(NBINS):
            col, row = b // 5, b % 5
            table = rate_here if row < 4 else rate_next
            local.append(pick(table, col - f, 15 * f + row % 4))

    outs = []
    for xb in range(CX // 8):
        bins = bins_of(xb)
        rated = []
        for f in range(2):
            value = jnp.zeros((8, 128), f32)
            for b in range(NBINS):
                value = jnp.where(bins[f] == b, local[10 * f + b], value)
            rated.append(value)
        own = slice(8 * xb, 8 * xb + 8)
        for g in range(4):
            turned = [roll(value, 32 * g) for value in rated]
            for z in range(4 * g, 4 * g + 4):
                for axis in range(3):
                    mix = turned[0] * flux[0, axis, z, own, :] + turned[1] * flux[1, axis, z, own, :]
                    staged[axis, z, own, :] = roll(mix, -32 * g)
        copy = pltpu.make_async_copy(staged.at[:, :, own], fine.at[:, :, own], out_sem.at[xb])
        copy.start()
        outs.append(copy)

    for d in order[2:]:
        to_column[d].wait_recv()
    crossed = [across_gx(rows_of(i)) for i in range(gy)]
    found = [jnp.zeros((gx, 128), f32) for _ in range(8)]
    half = (columns // 2) << row_bits
    for i in range(gy):
        rate, valid = rates_of(crossed[i], crossed[i - 1])
        pair = family * half + (row_full << row_bits) + 4 * i + row_bin
        pair = jnp.where(valid, pair, -1)
        for j in range(8):
            found[j] += jnp.where(pair == owned[j], rate, 0.0)
    line = jnp.zeros((1, 128), f32)
    for j in range(8):
        value = jnp.sum(jnp.sum(found[j], axis=0, keepdims=True), axis=1, keepdims=True)
        line += jnp.where(lane_row == j, value, 0.0)
    coarse[...] = line[:, :8]

    for d in order:
        to_column[d].wait_send()
    for copy in outs:
        copy.wait()


def solution(mesh):
    gx, gy = mesh.shape["gx"], mesh.shape["gy"]

    def shards(conductivity, well_rates, block_label, owned_pairs):
        vmem, dma = pltpu.VMEM, pltpu.SemaphoreType.DMA
        any_space = pl.BlockSpec(memory_space=pl.ANY)
        fine, coarse = pl.pallas_call(
            functools.partial(kernel, gx, gy),
            name="basis_flux",
            out_shape=(
                jax.ShapeDtypeStruct((3, NZ, CX, CY), f32),
                jax.ShapeDtypeStruct((1, 8), f32),
            ),
            in_specs=[any_space, any_space, any_space, pl.BlockSpec(memory_space=pltpu.SMEM)],
            out_specs=(any_space, pl.BlockSpec(memory_space=pltpu.VMEM)),
            scratch_shapes=[
                vmem((NZ, EXT, CY), f32),
                vmem((EXT, CY), jnp.int32),
                vmem((NZ, CX, CY), f32),
                vmem((3, CX, CY), f32),
                vmem((3, CX, CY), f32),
                vmem((3, EXT, CY), f32),
                vmem((3, EXT, CY), f32),
                vmem((20, ROWS, 128), f32),
                vmem((2, 5, ROWS, 128), jnp.int32),
                vmem((2, 20, ROWS, 128), f32),
                vmem((2, 20, ROWS, 128), f32),
                vmem((2, 20, ROWS, 128), f32),
                vmem((20, ROWS, 128), f32),
                vmem((5, ROWS, 128), f32),
                vmem((2, 20, ROWS, 128), f32),
                vmem((2, 5, ROWS, 128), f32),
                vmem((2, 2, 20, ROWS, 128), f32),
                vmem((2, 3, NZ, CX, CY), f32),
                vmem((2, 2, CX, CY), f32),
                vmem((1, 1, 128), f32),
                vmem((gx * gy, 1, 128), f32),
                vmem((3, NZ, CX, CY), f32),
                dma((3,)),
                dma((CX // 8,)),
                dma((10,)),
                dma((10,)),
                dma((gx,)),
                dma((gx,)),
                dma((gy,)),
                dma((gy,)),
            ],
            compiler_params=pltpu.CompilerParams(
                collective_id=0, has_side_effects=True, vmem_limit_bytes=60 * 1024 * 1024
            ),
        )(conductivity, well_rates, block_label, owned_pairs)
        return fine, coarse.reshape(8)

    in_specs = (P(None, "gx", "gy"), P(None, "gx", "gy"), P("gx", "gy"), P(("gx", "gy")))
    out_specs = (P(None, None, "gx", "gy"), P(("gx", "gy")))
    return jax.shard_map(shards, mesh=mesh, in_specs=in_specs, out_specs=out_specs, check_vma=False)
```

```python
import functools

import jax
import jax.numpy as jnp
from jax import lax
from jax.experimental import pallas as pl
from jax.experimental.pallas import tpu as pltpu
from jax.sharding import PartitionSpec as P

ITERS = 13
REACTION = 0.05
RELAXATION = 0.8
NZ = 16
CX = 64
CY = 128
HALO = 16
EXT = CX + 2 * HALO
PAD = 8
ROWS = EXT + 2 * PAD
PHASES = 5
NV = 4 * PHASES
NBINS = 10
MESH = pl.DeviceIdType.MESH
f32 = jnp.float32


def lane_iota():
    return lax.broadcasted_iota(jnp.int32, (8, 128), 1)


def roll(value, shift):
    return pltpu.roll(value, shift % 128, 1)


def take(value, lanes):
    return jnp.take_along_axis(value, lanes, axis=1, mode="promise_in_bounds")


def rows8(start):
    return pl.ds(pl.multiple_of(start, 8), 8)


def right_of(v, i):
    k, f = divmod(i, PHASES)
    return v[i + 1] if f < PHASES - 1 else roll(v[PHASES * k], -1)


def left_of(v, i):
    k, f = divmod(i, PHASES)
    return v[i - 1] if f > 0 else roll(v[PHASES * k + PHASES - 1], 1)


def above_of(v, i):
    k, f = divmod(i, PHASES)
    return v[i + PHASES] if k < 3 else roll(v[f], -32)


def below_of(v, i):
    k, f = divmod(i, PHASES)
    return v[i - PHASES] if k > 0 else roll(v[3 * PHASES + f], 32)


class Lanes:
    def __init__(self, residue=None):
        lane = lane_iota()
        self.lane = lane
        self.group = lane >> 5
        self.inner = lane & 31
        if residue is None:
            residue = [((lane - 2 * g) & 127) % PHASES for g in range(4)]
        self.residue = residue

    def column(self, f):
        return PHASES * self.inner + f

    def outside(self, f):
        y = self.column(f)
        return (y < HALO) | (y >= HALO + CY)

    def main(self, f):
        return (self.column(f) - HALO + 2 * self.group) & 127

    def plain(self, f):
        return (self.column(f) - HALO) & 127

    def strip(self, f):
        y = self.column(f)
        return (32 * self.group + jnp.where(y < HALO, y - HALO, y - HALO - CY)) & 127

    def back(self, f):
        found = jnp.zeros_like(self.lane)
        for g in range(4):
            y = (self.lane - 2 * g) & 127
            j = (y + HALO - f) // PHASES
            found = jnp.where(self.residue[g] == (f + 4) % PHASES, 32 * g + j, found)
        return found

    def spread(self, natural, tables):
        out = []
        for k in range(4):
            turned = [roll(natural[4 * g + k], 2 * g) if g else natural[k] for g in range(4)]
            for f in range(PHASES):
                merged = turned[0]
                for g in range(1, 4):
                    merged = jnp.where(self.residue[g] == (f + 4) % PHASES, turned[g], merged)
                out.append(take(merged, tables[f]))
        return out

    def gather_back(self, phases, tables):
        out = [None] * NZ
        for k in range(4):
            moved = [take(phases[PHASES * k + f], tables[f]) for f in range(PHASES)]
            for g in range(4):
                merged = moved[0]
                for f in range(1, PHASES):
                    merged = jnp.where(self.residue[g] == (f + 4) % PHASES, moved[f], merged)
                out[4 * g + k] = roll(merged, -2 * g) if g else merged
        return out

    def compose(self, own):
        around = ((self.lane + 16) & 127) >> 5
        low = jnp.where(around < 1, own[0], own[1])
        return jnp.where(around < 2, low, jnp.where(around < 3, own[2], own[3]))

    def squeeze(self, v):
        even, low = (self.group & 1) == 0, self.group < 2
        return jnp.where(low, jnp.where(even, v[0], v[1]), jnp.where(even, v[2], v[3]))

    def fold(self, v):
        even, low = (self.group & 1) == 0, self.group < 2
        halves = []
        for a, b in ((v[0], v[1]), (v[2], v[3])):
            halves.append(jnp.where(even, a, b) + roll(jnp.where(even, b, a), -32))
        four = jnp.where(low, halves[0], halves[1]) + roll(jnp.where(low, halves[1], halves[0]), -64)
        last = v[4] + roll(v[4], 32)
        return four, last + roll(last, 64)


def harmonic(one, other):
    return 2.0 * one * other / (one + other)


def pair_ids(label, row_bits, columns):
    column = label >> row_bits
    row = label & ((1 << row_bits) - 1)
    first = ((column >> 1) << row_bits) + row
    second = ((((column + columns - 1) & (columns - 1)) >> 1) << row_bits) + row + ((columns // 2) << row_bits)
    sign = jnp.where((column & 1) == 0, 1.0, -1.0).astype(f32)
    return first, second, sign


def kernel(gx, gy, cond, well, label, owned, fine, coarse, ce, le, wl, send_l, send_r, from_l, from_r, tables,
           c, tags, ids, tx, ty, tyb, hz, w, signs, s, p, wells, flux, sums, natural, part, gathered,
           local_sem, halo_send, halo_recv, row_send, row_recv, col_send, col_recv):
    m, n = lax.axis_index("gx"), lax.axis_index("gy")
    row_bits = (4 * gy).bit_length() - 1
    columns = 2 * gx

    def at(dm, dn):
        return (lax.rem(m + dm + gx, gx), lax.rem(n + dn + gy, gy))

    partners = [at(d, 0) for d in range(1, gx)] + [at(0, d) for d in range(1, gy)]
    partners += [at(a, b) for a in (-1, 1) for b in (-1, 1)]
    barrier = pltpu.get_barrier_semaphore()
    for partner in partners:
        pl.semaphore_signal(barrier, inc=1, device_id=partner, device_id_type=MESH)

    own_rows = pl.ds(HALO, CX)
    loads = [
        pltpu.make_async_copy(cond, ce.at[:, own_rows], local_sem.at[0]),
        pltpu.make_async_copy(label, le.at[own_rows], local_sem.at[1]),
        pltpu.make_async_copy(well, wl, local_sem.at[2]),
    ]
    for load in loads:
        load.start()

    for f in range(2):
        tx[f, :, :PAD, :] = jnp.zeros((NV, PAD, 128), f32)
        for slot in range(2):
            p[slot, f, :, :PAD, :] = jnp.zeros((NV, PAD, 128), f32)
            p[slot, f, :, ROWS - PAD :, :] = jnp.zeros((NV, PAD, 128), f32)
        ids[f, :, ROWS - PAD :, :] = jnp.zeros((PHASES, PAD, 128), jnp.int32)
    c[:, ROWS - PAD :, :] = jnp.ones((NV, PAD, 128), f32)
    lanes = Lanes()
    for f in range(PHASES):
        tables[0, f] = lanes.main(f)
        tables[1, f] = lanes.strip(f)
        tables[2, f] = lanes.plain(f)
        tables[3, f] = lanes.back(f)
    for g in range(4):
        tables[4, g] = lanes.residue[g]

    loads[0].wait()
    loads[1].wait()

    def pack(xb, carry):
        lanes = Lanes()
        rows, out = rows8(HALO + 8 * xb), rows8(8 * xb)
        right_half = lanes.inner < 16
        mixed = [
            lanes.compose([roll(ce[4 * g + k, rows, :], 32 * g) for g in range(4)]) for k in range(4)
        ]
        for h in range(2):
            even, odd = mixed[2 * h], roll(mixed[2 * h + 1], 16)
            send_l[h, out, :] = jnp.where(right_half, even, odd)
            send_r[h, out, :] = jnp.where(right_half, odd, even)
        own = le[rows, :].astype(f32)
        marks = lanes.compose([roll(own, 32 * g) for g in range(4)])
        send_l[2, out, :] = marks
        send_r[2, out, :] = marks
        return carry

    lax.fori_loop(0, CX // 8, pack, 0)
    pl.semaphore_wait(barrier, len(partners))

    low, high = pl.ds(0, HALO), pl.ds(CX - HALO, HALO)
    below, above = pl.ds(0, HALO), pl.ds(HALO + CX, HALO)
    moves = [
        (cond.at[:, low], ce.at[:, above], at(-1, 0)),
        (cond.at[:, high], ce.at[:, below], at(1, 0)),
        (label.at[low], le.at[above], at(-1, 0)),
        (label.at[high], le.at[below], at(1, 0)),
        (send_l, from_r.at[:, own_rows], at(0, -1)),
        (send_r, from_l.at[:, own_rows], at(0, 1)),
        (send_l.at[:, low], from_r.at[:, above], at(-1, -1)),
        (send_l.at[:, high], from_r.at[:, below], at(1, -1)),
        (send_r.at[:, low], from_l.at[:, above], at(-1, 1)),
        (send_r.at[:, high], from_l.at[:, below], at(1, 1)),
    ]
    halos = [
        pltpu.make_async_remote_copy(src, dst, halo_send.at[i], halo_recv.at[i], device_id=to, device_id_type=MESH)
        for i, (src, dst, to) in enumerate(moves)
    ]
    for halo in halos:
        halo.start()

    def spread_own(xb, carry):
        lanes = Lanes([tables[4, g] for g in range(4)])
        rows, out = rows8(8 * xb), rows8(PAD + 8 * xb)
        main = [tables[0, f] for f in range(PHASES)]
        for i, value in enumerate(lanes.spread([ce[z, rows, :] for z in range(NZ)], main)):
            c[i, out, :] = value
        own = le[rows, :].astype(f32)
        for f in range(PHASES):
            tags[f, out, :] = take(own, tables[2, f])
        return carry

    def spread_wells(xb, carry):
        lanes = Lanes([tables[4, g] for g in range(4)])
        rows = rows8(8 * xb)
        main = [tables[0, f] for f in range(PHASES)]
        for i, value in enumerate(lanes.spread([wl[z, rows, :] for z in range(NZ)], main)):
            wells[i, rows, :] = value
        return carry

    lax.fori_loop(HALO // 8, (HALO + CX) // 8, spread_own, 0)
    loads[2].wait()
    lax.fori_loop(0, CX // 8, spread_wells, 0)
    for halo in halos:
        halo.wait()
    lax.fori_loop(0, HALO // 8, spread_own, 0)
    lax.fori_loop((HALO + CX) // 8, EXT // 8, spread_own, 0)

    def add_strips(xb, carry):
        lanes = Lanes()
        rows, out = rows8(8 * xb), rows8(PAD + 8 * xb)
        right_half = lanes.inner < 16
        strips = []
        for h in range(2):
            right, left = from_r[h, rows, :], from_l[h, rows, :]
            strips.append(jnp.where(right_half, right, left))
            strips.append(roll(jnp.where(right_half, left, right), -16))
        marks = jnp.where(right_half, from_r[2, rows, :], from_l[2, rows, :])
        for f in range(PHASES):
            outside, table = lanes.outside(f), tables[1, f]
            for k in range(4):
                i = PHASES * k + f
                c[i, out, :] = jnp.where(outside, take(strips[k], table), c[i, out, :])
            tag = jnp.where(outside, take(marks, table), tags[f, out, :]).astype(jnp.int32)
            first, second, sign = pair_ids(tag, row_bits, columns)
            ids[0, f, out, :] = first
            ids[1, f, out, :] = second
            s[f, out, :] = sign
        return carry

    lax.fori_loop(0, EXT // 8, add_strips, 0)

    def faces(xb, carry):
        group = lane_iota() >> 5
        a = PAD + 8 * xb
        here, ahead = rows8(a), pl.ds(a + 1, 8)
        cs = [c[i, here, :] for i in range(NV)]
        hx = [harmonic(cs[i], c[i, ahead, :]) for i in range(NV)]
        hy = [harmonic(cs[i], right_of(cs, i)) for i in range(NV)]
        for i in range(NV):
            face = harmonic(cs[i], above_of(cs, i))
            if i >= 3 * PHASES:
                face = jnp.where(group == 3, 0.0, face)
                hz[i - 3 * PHASES, here, :] = roll(face, 32)
            hz[PHASES + i, here, :] = face
        for f in range(2):
            pid = [ids[f, phase, here, :] for phase in range(PHASES)]
            same_x = [pid[phase] == ids[f, phase, ahead, :] for phase in range(PHASES)]
            same_y = [pid[phase] == right_of(pid, phase) for phase in range(PHASES)]
            tys = [jnp.where(same_y[i % PHASES], hy[i], 0.0) for i in range(NV)]
            for i in range(NV):
                tx[f, i, here, :] = jnp.where(same_x[i % PHASES], hx[i], 0.0)
                ty[f, i, here, :] = tys[i]
                if i % PHASES == 0:
                    tyb[f, i // PHASES, here, :] = left_of(tys, i)
        return carry

    lax.fori_loop(0, EXT // 8, faces, 0)

    def weights(it, carry):
        f, xb = it & 1, it >> 1
        a = PAD + 8 * xb
        here, behind = rows8(a), pl.ds(a - 1, 8)
        turn = jnp.where(f == 0, 1.0, -1.0).astype(f32)
        for phase in range(PHASES):
            source = turn * s[phase, here, :]
            signs[f, phase, here, :] = source
            for k in range(4):
                i = PHASES * k + phase
                left = tyb[f, k, here, :] if phase == 0 else ty[f, i - 1, here, :]
                total = REACTION + tx[f, i, here, :] + tx[f, i, behind, :] + ty[f, i, here, :] + left
                total += hz[PHASES + i, here, :] + hz[i, here, :]
                scale = RELAXATION / total
                w[f, i, here, :] = scale
                p[0, f, i, here, :] = source * scale
        return carry

    lax.fori_loop(0, 2 * (EXT // 8), weights, 0)

    def relax(src, f, a, ups):
        here, ahead, behind = pl.ds(a, 8), pl.ds(a + 1, 8), pl.ds(a - 1, 8)
        ps = [p[src, f, i, here, :] for i in range(NV)]
        tys = [ty[f, i, here, :] for i in range(NV)]
        for i in range(NV):
            k, phase = divmod(i, PHASES)
            total = signs[f, phase, here, :] + tx[f, i, here, :] * p[src, f, i, ahead, :]
            total += tx[f, i, behind, :] * p[src, f, i, behind, :]
            total += tys[i] * right_of(ps, i)
            total += (tys[i - 1] if phase > 0 else tyb[f, k, here, :]) * left_of(ps, i)
            total += ups[PHASES + i] * above_of(ps, i)
            total += ups[i] * below_of(ps, i)
            p[1 - src, f, i, here, :] = (1.0 - RELAXATION) * ps[i] + w[f, i, here, :] * total

    def sweep(src, first, last):
        def step(xb, carry):
            a = PAD + first + 8 * xb
            ups = [hz[i, pl.ds(a, 8), :] for i in range(NV + PHASES)]
            relax(src, 0, a, ups)
            relax(src, 1, a, ups)
            return carry

        lax.fori_loop(0, -(-(last - first) // 8), step, 0)

    for k in range(2, ITERS + 1):
        first = HALO - (ITERS - k)
        last = HALO + CX + (ITERS - k) + 1
        sweep(k % 2, first, last)
    done = (ITERS + 1) % 2

    def fluxes(it, carry):
        f, xb = it & 1, it >> 1
        lanes = Lanes()
        a = PAD + HALO + 8 * xb
        here, ahead, own = rows8(a), pl.ds(a + 1, 8), rows8(8 * xb)
        ps = [p[done, f, i, here, :] for i in range(NV)]
        energy, load = [None] * PHASES, [None] * PHASES
        for i in range(NV):
            phase = i % PHASES
            dx = ps[i] - p[done, f, i, ahead, :]
            dy = ps[i] - right_of(ps, i)
            dz = ps[i] - above_of(ps, i)
            vx = tx[f, i, here, :] * dx
            vy = ty[f, i, here, :] * dy
            vz = hz[PHASES + i, here, :] * dz
            flux[f, 0, i, own, :] = vx
            flux[f, 1, i, own, :] = vy
            flux[f, 2, i, own, :] = vz
            cell = vx * dx + vy * dy + vz * dz + REACTION * ps[i] * ps[i]
            rated = wells[i, own, :] * ps[i]
            energy[phase] = cell if i < PHASES else energy[phase] + cell
            load[phase] = rated if i < PHASES else load[phase] + rated
        for q, value in enumerate((energy, load)):
            four, last = lanes.fold(value)
            sums[f, q, 0, own, :] = four
            sums[f, q, 1, own, :] = last
        return carry

    lax.fori_loop(0, 2 * (CX // 8), fluxes, 0)

    def bins_of(marks):
        column = ((marks >> row_bits) - 2 * m) & (columns - 1)
        row = ((marks & ((1 << row_bits) - 1)) - 4 * n) & ((1 << row_bits) - 1)
        return [jnp.where(column >= edge, 5, 0) + row for edge in (2, 1)]

    lanes = Lanes()
    inside = [lanes.squeeze([jnp.where(lanes.outside(f), 0, 1) for f in range(4)]),
              jnp.where(lanes.outside(4) | (lanes.group > 0), 0, 1)]
    totals = [[[jnp.zeros((8, 128), f32) for _ in range(NBINS)] for _ in range(2)] for _ in range(2)]
    for xb in range(CX // 8):
        at_rows = slice(PAD + HALO + 8 * xb, PAD + HALO + 8 * xb + 8)
        marks = [tags[f, at_rows, :] for f in range(PHASES)]
        for half, mark in enumerate((lanes.squeeze(marks), marks[4])):
            bins = bins_of(mark.astype(jnp.int32))
            for f in range(2):
                index = jnp.where(inside[half] == 1, bins[f], -1)
                cells = [sums[f, q, half, 8 * xb : 8 * xb + 8, :] for q in range(2)]
                for b in range(NBINS):
                    hit = index == b
                    for q in range(2):
                        totals[q][f][b] += jnp.where(hit, cells[q], 0.0)
    lines = jnp.zeros((8, 128), f32)
    for q in range(2):
        for f in range(2):
            for b in range(NBINS):
                value = jnp.sum(totals[q][f][b], axis=1, keepdims=True)
                lines = jnp.where(lanes.lane == 20 * q + 10 * f + b, value, lines)
    line = jnp.sum(lines, axis=0, keepdims=True)
    part[0] = line
    mine = n * gx + m
    gathered[pl.ds(mine, 1)] = line[None]

    to_row = [
        pltpu.make_async_remote_copy(
            part, gathered.at[pl.ds(mine, 1)], row_send.at[d], row_recv.at[d], device_id=at(d, 0), device_id_type=MESH
        )
        for d in range(1, gx)
    ]
    for copy in to_row:
        copy.start()

    def return_fluxes(it, carry):
        lanes = Lanes([tables[4, g] for g in range(4)])
        own, t = rows8(8 * (it // 3)), it % 3
        back = [tables[3, phase] for phase in range(PHASES)]
        for f in range(2):
            out = lanes.gather_back([flux[f, t, i, own, :] for i in range(NV)], back)
            for z in range(NZ):
                natural[f, t, z, own, :] = out[z]
        return carry

    steps = 3 * (CX // 8)
    lax.fori_loop(0, steps // 2, return_fluxes, 0)
    for copy in to_row:
        copy.wait()
    block = pl.ds(n * gx, gx)
    order = sorted(range(1, gy), key=lambda d: min(d, gy - d))
    to_column = {
        d: pltpu.make_async_remote_copy(
            gathered.at[block], gathered.at[block], col_send.at[d], col_recv.at[d], device_id=at(0, d), device_id_type=MESH
        )
        for d in order
    }
    for d in order:
        to_column[d].start()
    lax.fori_loop(steps // 2, steps, return_fluxes, 0)

    lane_full = lax.broadcasted_iota(jnp.int32, (gx, 128), 1)
    row_full = lax.broadcasted_iota(jnp.int32, (gx, 128), 0)
    entry = lane_full % 20
    family = entry // 10
    column_bin = (entry // 5) & 1
    row_bin = entry % 5

    def rows_of(at_n):
        return jnp.concatenate([gathered[at_n * gx + i] for i in range(gx)], axis=0)

    def across_gx(value):
        before = pltpu.roll(pltpu.roll(value, 1, 0), 128 - 5, 1)
        after = pltpu.roll(pltpu.roll(value, gx - 1, 0), 5, 1)
        return value + jnp.where(family == 0, before, after)

    def rates_of(value, previous):
        whole = value + jnp.where(row_bin == 0, pltpu.roll(previous, 128 - 4, 1), 0.0)
        load = pltpu.roll(whole, 128 - 20, 1)
        valid = (lane_full < 20) & (column_bin == family) & (row_bin < 4)
        return jnp.where(valid, load / jnp.where(valid, whole, 1.0), 0.0), valid

    to_column[1].wait_recv()
    to_column[gy - 1].wait_recv()
    around = [across_gx(rows_of(lax.rem(n + d + gy, gy))) for d in (-1, 0, 1)]
    near = [rates_of(around[1], around[0])[0], rates_of(around[2], around[1])[0]]

    def pick_row(table, dm):
        hit = row_full == lax.rem(m + dm + gx, gx)
        return jnp.sum(jnp.where(hit, table, 0.0), axis=0, keepdims=True)

    picked = {(t, dm): pick_row(near[t], dm) for t in range(2) for dm in (-1, 0, 1)}
    local = []
    for f in range(2):
        for b in range(NBINS):
            col, row = b // 5, b % 5
            lane = 15 * f + row % 4
            local.append(picked[row // 4, col - f][:, lane : lane + 1])

    def mix(xb, carry):
        own = rows8(8 * xb)
        bins = bins_of(le[rows8(HALO + 8 * xb), :])
        rated = []
        for f in range(2):
            value = jnp.zeros((8, 128), f32)
            for b in range(NBINS):
                value = jnp.where(bins[f] == b, local[10 * f + b], value)
            rated.append(value)
        for z in range(NZ):
            for axis in range(3):
                fine[axis, z, own, :] = rated[0] * natural[0, axis, z, own, :] + rated[1] * natural[1, axis, z, own, :]
        return carry

    lax.fori_loop(0, CX // 8, mix, 0)

    for d in order[2:]:
        to_column[d].wait_recv()
    crossed = [across_gx(rows_of(i)) for i in range(gy)]
    found = [jnp.zeros((gx, 128), f32) for _ in range(8)]
    half = (columns // 2) << row_bits
    for i in range(gy):
        rate, valid = rates_of(crossed[i], crossed[i - 1])
        pair = family * half + (row_full << row_bits) + 4 * i + row_bin
        pair = jnp.where(valid, pair, -1)
        for j in range(8):
            found[j] += jnp.where(pair == owned[j], rate, 0.0)
    lines = jnp.zeros((gx, 128), f32)
    for j in range(8):
        value = jnp.sum(found[j], axis=1, keepdims=True)
        lines = jnp.where(lane_full == j, value, lines)
    coarse[...] = jnp.sum(lines, axis=0, keepdims=True)[:, :8]

    for d in order:
        to_column[d].wait_send()


def solution(mesh):
    gx, gy = mesh.shape["gx"], mesh.shape["gy"]

    def shards(conductivity, well_rates, block_label, owned_pairs):
        vmem, dma = pltpu.VMEM, pltpu.SemaphoreType.DMA
        any_space = pl.BlockSpec(memory_space=pl.ANY)
        fine, coarse = pl.pallas_call(
            functools.partial(kernel, gx, gy),
            name="basis_flux",
            out_shape=(
                pltpu.VMEM((3, NZ, CX, CY), f32),
                jax.ShapeDtypeStruct((1, 8), f32),
            ),
            in_specs=[any_space, any_space, any_space, pl.BlockSpec(memory_space=pltpu.SMEM)],
            out_specs=(pl.BlockSpec(memory_space=pltpu.VMEM), pl.BlockSpec(memory_space=pltpu.VMEM)),
            scratch_shapes=[
                vmem((NZ, EXT, CY), f32),
                vmem((EXT, CY), jnp.int32),
                vmem((NZ, CX, CY), f32),
                vmem((3, CX, CY), f32),
                vmem((3, CX, CY), f32),
                vmem((3, EXT, CY), f32),
                vmem((3, EXT, CY), f32),
                vmem((5, PHASES, 8, 128), jnp.int32),
                vmem((NV, ROWS, 128), f32),
                vmem((PHASES, ROWS, 128), f32),
                vmem((2, PHASES, ROWS, 128), jnp.int32),
                vmem((2, NV, ROWS, 128), f32),
                vmem((2, NV, ROWS, 128), f32),
                vmem((2, 4, ROWS, 128), f32),
                vmem((NV + PHASES, ROWS, 128), f32),
                vmem((2, NV, ROWS, 128), f32),
                vmem((2, PHASES, ROWS, 128), f32),
                vmem((PHASES, ROWS, 128), f32),
                vmem((2, 2, NV, ROWS, 128), f32),
                vmem((NV, CX, 128), f32),
                vmem((2, 3, NV, CX, 128), f32),
                vmem((2, 2, 2, CX, 128), f32),
                vmem((2, 3, NZ, CX, CY), f32),
                vmem((1, 1, 128), f32),
                vmem((gx * gy, 1, 128), f32),
                dma((3,)),
                dma((10,)),
                dma((10,)),
                dma((gx,)),
                dma((gx,)),
                dma((gy,)),
                dma((gy,)),
            ],
            compiler_params=pltpu.CompilerParams(
                collective_id=0, has_side_effects=True, vmem_limit_bytes=65_400_000
            ),
        )(conductivity, well_rates, block_label, owned_pairs)
        return fine, coarse.reshape(8)

    in_specs = (P(None, "gx", "gy"), P(None, "gx", "gy"), P("gx", "gy"), P(("gx", "gy")))
    out_specs = (P(None, None, "gx", "gy"), P(("gx", "gy")))
    return jax.shard_map(shards, mesh=mesh, in_specs=in_specs, out_specs=out_specs, check_vma=False)
```

```python
import functools

import jax
import jax.numpy as jnp
from jax import lax
from jax.experimental import pallas as pl
from jax.experimental.pallas import tpu as pltpu
from jax.sharding import PartitionSpec as P

ITERS = 13
REACTION = 0.05
RELAXATION = 0.8
NZ = 16
CX = 64
CY = 128
HALO = 16
EXT = CX + 2 * HALO
PAD = 8
ROWS = EXT + 2 * PAD
PHASES = 5
NV = 4 * PHASES
NBINS = 10
MESH = pl.DeviceIdType.MESH
f32 = jnp.float32


def lane_iota():
    return lax.broadcasted_iota(jnp.int32, (8, 128), 1)


def roll(value, shift):
    return pltpu.roll(value, shift % 128, 1)


def take(value, lanes):
    return jnp.take_along_axis(value, lanes, axis=1, mode="promise_in_bounds")


def rows8(start):
    return pl.ds(pl.multiple_of(start, 8), 8)


def right_of(v, i):
    k, f = divmod(i, PHASES)
    return v[i + 1] if f < PHASES - 1 else roll(v[PHASES * k], -1)


def left_of(v, i):
    k, f = divmod(i, PHASES)
    return v[i - 1] if f > 0 else roll(v[PHASES * k + PHASES - 1], 1)


def above_of(v, i):
    k, f = divmod(i, PHASES)
    return v[i + PHASES] if k < 3 else roll(v[f], -32)


def below_of(v, i):
    k, f = divmod(i, PHASES)
    return v[i - PHASES] if k > 0 else roll(v[3 * PHASES + f], 32)


def each(low, high, body, step):
    def group(i, carry):
        for j in range(step):
            body(low + step * i + j, carry)
        return carry

    lax.fori_loop(0, (high - low) // step, group, 0)


class Lanes:
    def __init__(self, residue=None):
        lane = lane_iota()
        self.lane = lane
        self.group = lane >> 5
        self.inner = lane & 31
        if residue is None:
            residue = [((lane - 2 * g) & 127) % PHASES for g in range(4)]
        self.residue = residue

    def column(self, f):
        return PHASES * self.inner + f

    def outside(self, f):
        y = self.column(f)
        return (y < HALO) | (y >= HALO + CY)

    def main(self, f):
        return (self.column(f) - HALO + 2 * self.group) & 127

    def plain(self, f):
        return (self.column(f) - HALO) & 127

    def strip(self, f):
        y = self.column(f)
        return (32 * self.group + jnp.where(y < HALO, y - HALO, y - HALO - CY)) & 127

    def back(self, f):
        found = jnp.zeros_like(self.lane)
        for g in range(4):
            y = (self.lane - 2 * g) & 127
            j = (y + HALO - f) // PHASES
            found = jnp.where(self.residue[g] == (f + 4) % PHASES, 32 * g + j, found)
        return found

    def spread(self, natural, tables):
        out = []
        for k in range(4):
            turned = [roll(natural[4 * g + k], 2 * g) if g else natural[k] for g in range(4)]
            for f in range(PHASES):
                merged = turned[0]
                for g in range(1, 4):
                    merged = jnp.where(self.residue[g] == (f + 4) % PHASES, turned[g], merged)
                out.append(take(merged, tables[f]))
        return out

    def gather_back(self, phases, tables):
        out = [None] * NZ
        for k in range(4):
            moved = [take(phases[PHASES * k + f], tables[f]) for f in range(PHASES)]
            for g in range(4):
                merged = moved[0]
                for f in range(1, PHASES):
                    merged = jnp.where(self.residue[g] == (f + 4) % PHASES, moved[f], merged)
                out[4 * g + k] = roll(merged, -2 * g) if g else merged
        return out

    def compose(self, own):
        around = ((self.lane + 16) & 127) >> 5
        low = jnp.where(around < 1, own[0], own[1])
        return jnp.where(around < 2, low, jnp.where(around < 3, own[2], own[3]))

    def squeeze(self, v):
        even, low = (self.group & 1) == 0, self.group < 2
        return jnp.where(low, jnp.where(even, v[0], v[1]), jnp.where(even, v[2], v[3]))

    def fold(self, v):
        even, low = (self.group & 1) == 0, self.group < 2
        halves = []
        for a, b in ((v[0], v[1]), (v[2], v[3])):
            halves.append(jnp.where(even, a, b) + roll(jnp.where(even, b, a), -32))
        four = jnp.where(low, halves[0], halves[1]) + roll(jnp.where(low, halves[1], halves[0]), -64)
        last = v[4] + roll(v[4], 32)
        return four, last + roll(last, 64)


def harmonic(one, other):
    return 2.0 * one * other / (one + other)


def pair_ids(label, row_bits, columns):
    column = label >> row_bits
    row = label & ((1 << row_bits) - 1)
    first = ((column >> 1) << row_bits) + row
    second = ((((column + columns - 1) & (columns - 1)) >> 1) << row_bits) + row + ((columns // 2) << row_bits)
    sign = jnp.where((column & 1) == 0, 1.0, -1.0).astype(f32)
    return first, second, sign


def kernel(gx, gy, cond, well, label, owned, fine, coarse, ce, le, wl, send_l, send_r, from_l, from_r, tables,
           c, tags, ids, tx, ty, tyb, hz, w, signs, s, p, wells, flux, sums, natural, part, gathered,
           local_sem, halo_send, halo_recv, row_send, row_recv, col_send, col_recv):
    m, n = lax.axis_index("gx"), lax.axis_index("gy")
    row_bits = (4 * gy).bit_length() - 1
    columns = 2 * gx

    def at(dm, dn):
        return (lax.rem(m + dm + gx, gx), lax.rem(n + dn + gy, gy))

    partners = [at(d, 0) for d in range(1, gx)] + [at(0, d) for d in range(1, gy)]
    partners += [at(a, b) for a in (-1, 1) for b in (-1, 1)]
    barrier = pltpu.get_barrier_semaphore()
    for partner in partners:
        pl.semaphore_signal(barrier, inc=1, device_id=partner, device_id_type=MESH)

    own_rows = pl.ds(HALO, CX)
    loads = [
        pltpu.make_async_copy(cond, ce.at[:, own_rows], local_sem.at[0]),
        pltpu.make_async_copy(label, le.at[own_rows], local_sem.at[1]),
        pltpu.make_async_copy(well, wl, local_sem.at[2]),
    ]
    for load in loads:
        load.start()

    for f in range(2):
        tx[f, :, :PAD, :] = jnp.zeros((NV, PAD, 128), f32)
        for slot in range(2):
            p[slot, f, :, :PAD, :] = jnp.zeros((NV, PAD, 128), f32)
            p[slot, f, :, ROWS - PAD :, :] = jnp.zeros((NV, PAD, 128), f32)
        ids[f, :, ROWS - PAD :, :] = jnp.zeros((PHASES, PAD, 128), jnp.int32)
    c[:, ROWS - PAD :, :] = jnp.ones((NV, PAD, 128), f32)
    lanes = Lanes()
    for f in range(PHASES):
        tables[0, f] = lanes.main(f)
        tables[1, f] = lanes.strip(f)
        tables[2, f] = lanes.plain(f)
        tables[3, f] = lanes.back(f)
    for g in range(4):
        tables[4, g] = lanes.residue[g]

    loads[0].wait()
    loads[1].wait()

    def pack(xb, carry):
        lanes = Lanes()
        rows, out = rows8(HALO + 8 * xb), rows8(8 * xb)
        right_half = lanes.inner < 16
        mixed = [
            lanes.compose([roll(ce[4 * g + k, rows, :], 32 * g) for g in range(4)]) for k in range(4)
        ]
        for h in range(2):
            even, odd = mixed[2 * h], roll(mixed[2 * h + 1], 16)
            send_l[h, out, :] = jnp.where(right_half, even, odd)
            send_r[h, out, :] = jnp.where(right_half, odd, even)
        own = le[rows, :].astype(f32)
        marks = lanes.compose([roll(own, 32 * g) for g in range(4)])
        send_l[2, out, :] = marks
        send_r[2, out, :] = marks
        return carry

    each(0, CX // 8, pack, 4)
    pl.semaphore_wait(barrier, len(partners))

    low, high = pl.ds(0, HALO), pl.ds(CX - HALO, HALO)
    below, above = pl.ds(0, HALO), pl.ds(HALO + CX, HALO)
    moves = [
        (cond.at[:, low], ce.at[:, above], at(-1, 0)),
        (cond.at[:, high], ce.at[:, below], at(1, 0)),
        (label.at[low], le.at[above], at(-1, 0)),
        (label.at[high], le.at[below], at(1, 0)),
        (send_l, from_r.at[:, own_rows], at(0, -1)),
        (send_r, from_l.at[:, own_rows], at(0, 1)),
        (send_l.at[:, low], from_r.at[:, above], at(-1, -1)),
        (send_l.at[:, high], from_r.at[:, below], at(1, -1)),
        (send_r.at[:, low], from_l.at[:, above], at(-1, 1)),
        (send_r.at[:, high], from_l.at[:, below], at(1, 1)),
    ]
    halos = [
        pltpu.make_async_remote_copy(src, dst, halo_send.at[i], halo_recv.at[i], device_id=to, device_id_type=MESH)
        for i, (src, dst, to) in enumerate(moves)
    ]
    for halo in halos:
        halo.start()

    def spread_own(xb, carry):
        lanes = Lanes([tables[4, g] for g in range(4)])
        rows, out = rows8(8 * xb), rows8(PAD + 8 * xb)
        main = [tables[0, f] for f in range(PHASES)]
        for i, value in enumerate(lanes.spread([ce[z, rows, :] for z in range(NZ)], main)):
            c[i, out, :] = value
        own = le[rows, :].astype(f32)
        for f in range(PHASES):
            tags[f, out, :] = take(own, tables[2, f])
        return carry

    def spread_wells(xb, carry):
        lanes = Lanes([tables[4, g] for g in range(4)])
        rows = rows8(8 * xb)
        main = [tables[0, f] for f in range(PHASES)]
        for i, value in enumerate(lanes.spread([wl[z, rows, :] for z in range(NZ)], main)):
            wells[i, rows, :] = value
        return carry

    each(HALO // 8, (HALO + CX) // 8, spread_own, 4)
    loads[2].wait()
    each(0, CX // 8, spread_wells, 4)
    for halo in halos[:4]:
        halo.wait()
    each(0, HALO // 8, spread_own, 2)
    each((HALO + CX) // 8, EXT // 8, spread_own, 2)
    for halo in halos[4:]:
        halo.wait()

    def add_strips(xb, carry):
        lanes = Lanes()
        rows, out = rows8(8 * xb), rows8(PAD + 8 * xb)
        right_half = lanes.inner < 16
        strips = []
        for h in range(2):
            right, left = from_r[h, rows, :], from_l[h, rows, :]
            strips.append(jnp.where(right_half, right, left))
            strips.append(roll(jnp.where(right_half, left, right), -16))
        marks = jnp.where(right_half, from_r[2, rows, :], from_l[2, rows, :])
        for f in range(PHASES):
            outside, table = lanes.outside(f), tables[1, f]
            for k in range(4):
                i = PHASES * k + f
                c[i, out, :] = jnp.where(outside, take(strips[k], table), c[i, out, :])
            tag = jnp.where(outside, take(marks, table), tags[f, out, :]).astype(jnp.int32)
            first, second, sign = pair_ids(tag, row_bits, columns)
            ids[0, f, out, :] = first
            ids[1, f, out, :] = second
            s[f, out, :] = sign
        return carry

    each(0, EXT // 8, add_strips, 4)

    def faces(xb, carry):
        group = lane_iota() >> 5
        a = PAD + 8 * xb
        here, ahead = rows8(a), pl.ds(a + 1, 8)
        cs = [c[i, here, :] for i in range(NV)]
        hx = [harmonic(cs[i], c[i, ahead, :]) for i in range(NV)]
        hy = [harmonic(cs[i], right_of(cs, i)) for i in range(NV)]
        for i in range(NV):
            face = harmonic(cs[i], above_of(cs, i))
            if i >= 3 * PHASES:
                face = jnp.where(group == 3, 0.0, face)
                hz[i - 3 * PHASES, here, :] = roll(face, 32)
            hz[PHASES + i, here, :] = face
        for f in range(2):
            pid = [ids[f, phase, here, :] for phase in range(PHASES)]
            same_x = [pid[phase] == ids[f, phase, ahead, :] for phase in range(PHASES)]
            same_y = [pid[phase] == right_of(pid, phase) for phase in range(PHASES)]
            tys = [jnp.where(same_y[i % PHASES], hy[i], 0.0) for i in range(NV)]
            for i in range(NV):
                tx[f, i, here, :] = jnp.where(same_x[i % PHASES], hx[i], 0.0)
                ty[f, i, here, :] = tys[i]
                if i % PHASES == 0:
                    tyb[f, i // PHASES, here, :] = left_of(tys, i)
        return carry

    each(0, EXT // 8, faces, 2)

    def weights(it, carry):
        f, xb = it & 1, it >> 1
        a = PAD + 8 * xb
        here, behind = rows8(a), pl.ds(a - 1, 8)
        turn = jnp.where(f == 0, 1.0, -1.0).astype(f32)
        for phase in range(PHASES):
            source = turn * s[phase, here, :]
            signs[f, phase, here, :] = source
            for k in range(4):
                i = PHASES * k + phase
                left = tyb[f, k, here, :] if phase == 0 else ty[f, i - 1, here, :]
                total = REACTION + tx[f, i, here, :] + tx[f, i, behind, :] + ty[f, i, here, :] + left
                total += hz[PHASES + i, here, :] + hz[i, here, :]
                scale = RELAXATION / total
                w[f, i, here, :] = scale
                p[0, f, i, here, :] = source * scale
        return carry

    lax.fori_loop(0, 2 * (EXT // 8), weights, 0)

    def relax(src, f, a, ups):
        here, ahead, behind = pl.ds(a, 8), pl.ds(a + 1, 8), pl.ds(a - 1, 8)
        ps = [p[src, f, i, here, :] for i in range(NV)]
        tys = [ty[f, i, here, :] for i in range(NV)]
        for i in range(NV):
            k, phase = divmod(i, PHASES)
            total = signs[f, phase, here, :] + tx[f, i, here, :] * p[src, f, i, ahead, :]
            total += tx[f, i, behind, :] * p[src, f, i, behind, :]
            total += tys[i] * right_of(ps, i)
            total += (tys[i - 1] if phase > 0 else tyb[f, k, here, :]) * left_of(ps, i)
            total += ups[PHASES + i] * above_of(ps, i)
            total += ups[i] * below_of(ps, i)
            p[1 - src, f, i, here, :] = (1.0 - RELAXATION) * ps[i] + w[f, i, here, :] * total

    def sweep(src, first, last):
        def step(xb, carry):
            a = PAD + first + 8 * xb
            ups = [hz[i, pl.ds(a, 8), :] for i in range(NV + PHASES)]
            relax(src, 0, a, ups)
            relax(src, 1, a, ups)
            return carry

        lax.fori_loop(0, -(-(last - first) // 8), step, 0)

    for k in range(2, ITERS + 1):
        first = HALO - (ITERS - k)
        last = HALO + CX + (ITERS - k) + 1
        sweep(k % 2, first, last)
    done = (ITERS + 1) % 2

    def fluxes(it, carry):
        f, xb = it & 1, it >> 1
        lanes = Lanes()
        a = PAD + HALO + 8 * xb
        here, ahead, own = rows8(a), pl.ds(a + 1, 8), rows8(8 * xb)
        ps = [p[done, f, i, here, :] for i in range(NV)]
        energy, load = [None] * PHASES, [None] * PHASES
        for i in range(NV):
            phase = i % PHASES
            dx = ps[i] - p[done, f, i, ahead, :]
            dy = ps[i] - right_of(ps, i)
            dz = ps[i] - above_of(ps, i)
            vx = tx[f, i, here, :] * dx
            vy = ty[f, i, here, :] * dy
            vz = hz[PHASES + i, here, :] * dz
            flux[f, 0, i, own, :] = vx
            flux[f, 1, i, own, :] = vy
            flux[f, 2, i, own, :] = vz
            cell = vx * dx + vy * dy + vz * dz + REACTION * ps[i] * ps[i]
            rated = wells[i, own, :] * ps[i]
            energy[phase] = cell if i < PHASES else energy[phase] + cell
            load[phase] = rated if i < PHASES else load[phase] + rated
        for q, value in enumerate((energy, load)):
            four, last = lanes.fold(value)
            sums[f, q, 0, own, :] = four
            sums[f, q, 1, own, :] = last
        return carry

    each(0, 2 * (CX // 8), fluxes, 4)

    def bins_of(marks):
        column = ((marks >> row_bits) - 2 * m) & (columns - 1)
        row = ((marks & ((1 << row_bits) - 1)) - 4 * n) & ((1 << row_bits) - 1)
        return [jnp.where(column >= edge, 5, 0) + row for edge in (2, 1)]

    lanes = Lanes()
    inside = [lanes.squeeze([jnp.where(lanes.outside(f), 0, 1) for f in range(4)]),
              jnp.where(lanes.outside(4) | (lanes.group > 0), 0, 1)]
    totals = [[[jnp.zeros((8, 128), f32) for _ in range(NBINS)] for _ in range(2)] for _ in range(2)]
    for xb in range(CX // 8):
        at_rows = slice(PAD + HALO + 8 * xb, PAD + HALO + 8 * xb + 8)
        marks = [tags[f, at_rows, :] for f in range(PHASES)]
        for half, mark in enumerate((lanes.squeeze(marks), marks[4])):
            bins = bins_of(mark.astype(jnp.int32))
            for f in range(2):
                index = jnp.where(inside[half] == 1, bins[f], -1)
                cells = [sums[f, q, half, 8 * xb : 8 * xb + 8, :] for q in range(2)]
                for b in range(NBINS):
                    hit = index == b
                    for q in range(2):
                        totals[q][f][b] += jnp.where(hit, cells[q], 0.0)
    lines = jnp.zeros((8, 128), f32)
    for q in range(2):
        for f in range(2):
            for b in range(NBINS):
                value = jnp.sum(totals[q][f][b], axis=1, keepdims=True)
                lines = jnp.where(lanes.lane == 20 * q + 10 * f + b, value, lines)
    line = jnp.sum(lines, axis=0, keepdims=True)
    part[0] = line
    mine = n * gx + m
    gathered[pl.ds(mine, 1)] = line[None]

    to_row = [
        pltpu.make_async_remote_copy(
            part, gathered.at[pl.ds(mine, 1)], row_send.at[d], row_recv.at[d], device_id=at(d, 0), device_id_type=MESH
        )
        for d in range(1, gx)
    ]
    for copy in to_row:
        copy.start()

    def return_fluxes(it, carry):
        lanes = Lanes([tables[4, g] for g in range(4)])
        own, t = rows8(8 * (it // 3)), it % 3
        back = [tables[3, phase] for phase in range(PHASES)]
        for f in range(2):
            out = lanes.gather_back([flux[f, t, i, own, :] for i in range(NV)], back)
            for z in range(NZ):
                natural[f, t, z, own, :] = out[z]
        return carry

    steps = 3 * (CX // 8)
    each(0, steps // 2, return_fluxes, 2)
    for copy in to_row:
        copy.wait()
    block = pl.ds(n * gx, gx)
    order = sorted(range(1, gy), key=lambda d: min(d, gy - d))
    to_column = {
        d: pltpu.make_async_remote_copy(
            gathered.at[block], gathered.at[block], col_send.at[d], col_recv.at[d], device_id=at(0, d), device_id_type=MESH
        )
        for d in order
    }
    for d in order:
        to_column[d].start()
    each(steps // 2, steps, return_fluxes, 2)

    lane_full = lax.broadcasted_iota(jnp.int32, (gx, 128), 1)
    row_full = lax.broadcasted_iota(jnp.int32, (gx, 128), 0)
    entry = lane_full % 20
    family = entry // 10
    column_bin = (entry // 5) & 1
    row_bin = entry % 5

    def rows_of(at_n):
        return jnp.concatenate([gathered[at_n * gx + i] for i in range(gx)], axis=0)

    def across_gx(value):
        before = pltpu.roll(pltpu.roll(value, 1, 0), 128 - 5, 1)
        after = pltpu.roll(pltpu.roll(value, gx - 1, 0), 5, 1)
        return value + jnp.where(family == 0, before, after)

    def rates_of(value, previous):
        whole = value + jnp.where(row_bin == 0, pltpu.roll(previous, 128 - 4, 1), 0.0)
        load = pltpu.roll(whole, 128 - 20, 1)
        valid = (lane_full < 20) & (column_bin == family) & (row_bin < 4)
        return jnp.where(valid, load / jnp.where(valid, whole, 1.0), 0.0), valid

    to_column[1].wait_recv()
    to_column[gy - 1].wait_recv()
    around = [across_gx(rows_of(lax.rem(n + d + gy, gy))) for d in (-1, 0, 1)]
    near = [rates_of(around[1], around[0])[0], rates_of(around[2], around[1])[0]]

    def pick_row(table, dm):
        hit = row_full == lax.rem(m + dm + gx, gx)
        return jnp.sum(jnp.where(hit, table, 0.0), axis=0, keepdims=True)

    picked = {(t, dm): pick_row(near[t], dm) for t in range(2) for dm in (-1, 0, 1)}
    local = []
    for f in range(2):
        for b in range(NBINS):
            col, row = b // 5, b % 5
            lane = 15 * f + row % 4
            local.append(picked[row // 4, col - f][:, lane : lane + 1])

    def mix(xb, carry):
        own = rows8(8 * xb)
        bins = bins_of(le[rows8(HALO + 8 * xb), :])
        rated = []
        for f in range(2):
            value = jnp.zeros((8, 128), f32)
            for b in range(NBINS):
                value = jnp.where(bins[f] == b, local[10 * f + b], value)
            rated.append(value)
        for z in range(NZ):
            for axis in range(3):
                fine[axis, z, own, :] = rated[0] * natural[0, axis, z, own, :] + rated[1] * natural[1, axis, z, own, :]
        return carry

    lax.fori_loop(0, CX // 8, mix, 0)

    for d in order[2:]:
        to_column[d].wait_recv()
    crossed = [across_gx(rows_of(i)) for i in range(gy)]
    found = [jnp.zeros((gx, 128), f32) for _ in range(8)]
    half = (columns // 2) << row_bits
    for i in range(gy):
        rate, valid = rates_of(crossed[i], crossed[i - 1])
        pair = family * half + (row_full << row_bits) + 4 * i + row_bin
        pair = jnp.where(valid, pair, -1)
        for j in range(8):
            found[j] += jnp.where(pair == owned[j], rate, 0.0)
    lines = jnp.zeros((gx, 128), f32)
    for j in range(8):
        value = jnp.sum(found[j], axis=1, keepdims=True)
        lines = jnp.where(lane_full == j, value, lines)
    coarse[...] = jnp.sum(lines, axis=0, keepdims=True)[:, :8]

    for d in order:
        to_column[d].wait_send()


def solution(mesh):
    gx, gy = mesh.shape["gx"], mesh.shape["gy"]

    def shards(conductivity, well_rates, block_label, owned_pairs):
        vmem, dma = pltpu.VMEM, pltpu.SemaphoreType.DMA
        any_space = pl.BlockSpec(memory_space=pl.ANY)
        fine, coarse = pl.pallas_call(
            functools.partial(kernel, gx, gy),
            name="basis_flux",
            out_shape=(
                pltpu.VMEM((3, NZ, CX, CY), f32),
                jax.ShapeDtypeStruct((1, 8), f32),
            ),
            in_specs=[any_space, any_space, any_space, pl.BlockSpec(memory_space=pltpu.SMEM)],
            out_specs=(pl.BlockSpec(memory_space=pltpu.VMEM), pl.BlockSpec(memory_space=pltpu.VMEM)),
            scratch_shapes=[
                vmem((NZ, EXT, CY), f32),
                vmem((EXT, CY), jnp.int32),
                vmem((NZ, CX, CY), f32),
                vmem((3, CX, CY), f32),
                vmem((3, CX, CY), f32),
                vmem((3, EXT, CY), f32),
                vmem((3, EXT, CY), f32),
                vmem((5, PHASES, 8, 128), jnp.int32),
                vmem((NV, ROWS, 128), f32),
                vmem((PHASES, ROWS, 128), f32),
                vmem((2, PHASES, ROWS, 128), jnp.int32),
                vmem((2, NV, ROWS, 128), f32),
                vmem((2, NV, ROWS, 128), f32),
                vmem((2, 4, ROWS, 128), f32),
                vmem((NV + PHASES, ROWS, 128), f32),
                vmem((2, NV, ROWS, 128), f32),
                vmem((2, PHASES, ROWS, 128), f32),
                vmem((PHASES, ROWS, 128), f32),
                vmem((2, 2, NV, ROWS, 128), f32),
                vmem((NV, CX, 128), f32),
                vmem((2, 3, NV, CX, 128), f32),
                vmem((2, 2, 2, CX, 128), f32),
                vmem((2, 3, NZ, CX, CY), f32),
                vmem((1, 1, 128), f32),
                vmem((gx * gy, 1, 128), f32),
                dma((3,)),
                dma((10,)),
                dma((10,)),
                dma((gx,)),
                dma((gx,)),
                dma((gy,)),
                dma((gy,)),
            ],
            compiler_params=pltpu.CompilerParams(
                collective_id=0, has_side_effects=True, vmem_limit_bytes=65_400_000
            ),
        )(conductivity, well_rates, block_label, owned_pairs)
        return fine, coarse.reshape(8)

    in_specs = (P(None, "gx", "gy"), P(None, "gx", "gy"), P("gx", "gy"), P(("gx", "gy")))
    out_specs = (P(None, None, "gx", "gy"), P(("gx", "gy")))
    return jax.shard_map(shards, mesh=mesh, in_specs=in_specs, out_specs=out_specs, check_vma=False)
```
